32 devices in a mesh: shard: 8 (over z, y), pair: 4 (over x, core).
Axes of the slice: x: 2, y: 2, z: 4, core: 2. Of those that a mesh axis runs over, the one named last changes fastest.
Arguments:
- embeds: float32 [8192, 768], P(('shard', 'pair')), may hold values from -256 to 256
- cluster: int32 [8192], P(('shard', 'pair')), may hold values from 0 to 127, as said below
- rank: int32 [8192], P(('shard', 'pair')), may hold values from 0 to 8191, each once
Outputs:
- best: float32 [8192], P(('shard', 'pair'))
The draws below stay inside these ranges and needn't reach their ends.
Inputs may be any that keep to these rules, and one draw needn't show every extreme that they name: Among the rows of one device no group cluster // 16 is named more than 64 times and no quarter of a group more than 16 times; one group, the same for every device, is named exactly 64 times by the rows of every device, each of its quarters exactly 16 times. No two rows share a rank.
All inputs are finite; a program needn't handle non-finite values.
Results may differ from the reference program's by a relative error of at most 0.00031.
Values may be sent and summed in bfloat16 or wider, within the bound.
A program may use at most 64 MiB of HBM per device.

```python
import math
import jax
import jax.numpy as jnp
from jax import lax

D = 768
ROWS_DEV = 256
CL_OWN = 16
CLUSTERS = 128
ROWS = 8192
N_PAIR = 4


def layout_groups(key):
    base = jax.random.fold_in(key, 7)
    devices = ROWS // ROWS_DEV
    groups = CLUSTERS // CL_OWN
    capacity = 2 * ROWS_DEV // groups
    quarter_width = CL_OWN // N_PAIR
    heavy = jax.random.randint(jax.random.fold_in(base, 1), (), 0, groups)
    entries = jnp.arange(groups * capacity, dtype=jnp.int32)
    pool = entries // capacity
    quarter_of = entries % capacity * N_PAIR // capacity

    def one_device(index):
        device_key = jax.random.fold_in(base, index + 2)
        shuffled = jax.random.permutation(jax.random.fold_in(device_key, 0), groups * capacity).astype(jnp.int32)
        priority = jnp.where(pool == heavy, -1, shuffled)
        picked = jnp.argsort(priority, stable=True)[:ROWS_DEV]
        mixing = jax.random.permutation(jax.random.fold_in(device_key, 1), ROWS_DEV)
        homes = pool[picked][mixing]
        quarters = quarter_of[picked][mixing]
        member = jax.random.randint(jax.random.fold_in(device_key, 2), (ROWS_DEV,), 0, quarter_width)
        return (homes * CL_OWN + quarters * quarter_width + member).astype(jnp.int32)
    return jax.vmap(one_device)(jnp.arange(devices, dtype=jnp.int32)).reshape(ROWS)


def draw_cluster(key, part):
    return layout_groups(key)


def draw_embeds(key, part):
    cluster_ids = layout_groups(key)
    inner = jax.random.fold_in(key, 11)
    centers = jax.random.normal(jax.random.fold_in(inner, 0), (CLUSTERS, D), jnp.float32)
    weights = jax.random.uniform(jax.random.fold_in(inner, 1), (ROWS, 1), jnp.float32, 0.2, 2.0)
    scales = jnp.exp(jax.random.uniform(jax.random.fold_in(inner, 2), (ROWS, 1), jnp.float32, 0.0, math.log(10.0)))
    noise = jax.random.normal(jax.random.fold_in(inner, 3), (ROWS, D), jnp.float32)
    values = scales * (weights * centers[cluster_ids] + noise)
    return jnp.clip(values, -256.0, 256.0)


def setup_inputs(seed: int = 0) -> dict:
    streams_of = jax.random.split(jax.random.key(seed), 4)
    return {
        "embeds": draw_embeds(jax.random.fold_in(streams_of[3], 71), 0),
        "cluster": draw_cluster(jax.random.fold_in(streams_of[3], 71), 0),
        "rank": jax.random.permutation(streams_of[2], ROWS).astype(jnp.int32),
    }


def reference(embeds, cluster, rank):
    squares = lax.optimization_barrier(jnp.sum(embeds * embeds, axis=1, keepdims=True))
    unit_rows = (embeds * lax.rsqrt(squares + 1e-06)).astype(jnp.bfloat16)
    groups = CLUSTERS // CL_OWN
    window = 2 * ROWS_DEV * N_PAIR
    home_group = (cluster // CL_OWN).astype(jnp.int32)
    row_order = jnp.argsort(home_group, stable=True).astype(jnp.int32)
    sorted_home = home_group[row_order]
    starts = jnp.searchsorted(sorted_home, jnp.arange(groups, dtype=jnp.int32), side='left').astype(jnp.int32)
    pad_units = jnp.concatenate([unit_rows[row_order], jnp.zeros((window, D), jnp.bfloat16)], axis=0)
    pad_clusters = jnp.concatenate([cluster[row_order], jnp.full((window,), -1, jnp.int32)], axis=0)
    pad_ranks = jnp.concatenate([rank[row_order], jnp.zeros((window,), jnp.int32)], axis=0)

    def one_group(first):
        vectors = lax.dynamic_slice_in_dim(pad_units, first, window, 0).astype(jnp.float32)
        clusters = lax.dynamic_slice_in_dim(pad_clusters, first, window, 0)
        ranks = lax.dynamic_slice_in_dim(pad_ranks, first, window, 0)
        scores = jnp.dot(vectors, vectors.T, preferred_element_type=jnp.float32, precision=lax.Precision.HIGHEST)
        masked = (clusters[:, None] == clusters[None, :]) & (ranks[None, :] < ranks[:, None])
        return lax.optimization_barrier(jnp.max(jnp.where(masked, scores, -1.0), axis=1))
    results = lax.map(one_group, starts)
    position = jnp.arange(ROWS, dtype=jnp.int32) - starts[sorted_home]
    sorted_best = results.reshape(-1)[sorted_home * window + position]
    return jnp.zeros((ROWS,), jnp.float32).at[row_order].set(sorted_best)
```

```python
import functools

import jax
import jax.numpy as jnp
from jax import lax
from jax.experimental import pallas as pl
from jax.experimental.pallas import tpu as pltpu
from jax.sharding import PartitionSpec as P

CL_OWN = 16
LANES = 128
MESH = pl.DeviceIdType.MESH


def log2(value):
    return (value - 1).bit_length()


def kernel(
    pairs, sub, bits, step_bits,
    embeds_ref, cluster_ref, rank_ref, out_ref,
    send_u, recv_u, send_k, recv_k, answers, returned,
    u_send, u_recv, k_send, k_recv, a_send, a_recv,
):
    devices = recv_u.shape[0]
    rows, width = embeds_ref.shape
    slots = devices * sub
    per = LANES // sub
    chunks = devices // per
    me = lax.axis_index("shard") * pairs + lax.axis_index("pair")
    my_chunk = me // per
    my_place = me % per

    def coords(device):
        return (device // pairs, device % pairs)

    def copy_units(device):
        return pltpu.make_async_remote_copy(
            src_ref=send_u.at[device], dst_ref=recv_u.at[me],
            send_sem=u_send.at[device], recv_sem=u_recv.at[me],
            device_id=coords(device), device_id_type=MESH)

    def copy_keys(device):
        return pltpu.make_async_remote_copy(
            src_ref=send_k.at[device // per], dst_ref=recv_k.at[me],
            send_sem=k_send.at[device], recv_sem=k_recv.at[me],
            device_id=coords(device), device_id_type=MESH)

    def copy_answers(device):
        return pltpu.make_async_remote_copy(
            src_ref=answers.at[device // per], dst_ref=returned.at[me],
            send_sem=a_send.at[device], recv_sem=a_recv.at[me],
            device_id=coords(device), device_id_type=MESH)

    def await_from(device):
        def wait(buffer, send, recv):
            pltpu.make_async_remote_copy(
                src_ref=buffer.at[device], dst_ref=buffer.at[device],
                send_sem=send.at[device], recv_sem=recv.at[device],
                device_id=coords(device), device_id_type=MESH).wait_recv()
        return wait

    def others(action):
        def step(k, carry):
            action(lax.rem(me + k, devices))
            return carry
        lax.fori_loop(1, devices, step, 0)

    if chunks == 4:
        order = [3 - my_chunk, (my_chunk + 2) % 4, my_chunk + 1 - 2 * (my_chunk % 2), my_chunk]
    else:
        order = [(my_chunk + chunks // 2 + k) % chunks for k in range(chunks)]
        order = [c for c in order]

    barrier = pltpu.get_barrier_semaphore()
    others(lambda d: pl.semaphore_signal(barrier, inc=1, device_id=coords(d), device_id_type=MESH))

    cluster = cluster_ref[...]
    key = cluster * (1 << bits) + rank_ref[...]
    bucket = lax.shift_right_logical(cluster, step_bits)

    def columns(row):
        return jnp.transpose(jnp.broadcast_to(row, (LANES, row.shape[1])))

    bucket_column = columns(bucket)
    lower = lax.broadcasted_iota(jnp.int32, (rows, LANES), 0)
    lane = lax.broadcasted_iota(jnp.int32, (rows, LANES), 1)
    places = []
    for part in range(rows // LANES):
        here = bucket[:, part * LANES:(part + 1) * LANES]
        before = (bucket_column == here) & (lower < lane + part * LANES)
        places.append(jnp.sum(before.astype(jnp.int32), axis=0, keepdims=True))
    position = jnp.concatenate(places, axis=1)
    slot = bucket * sub + position
    slot_column = columns(slot)
    key_column = columns(key)
    for part in range(chunks):
        found = jnp.where(slot_column == lane + part * LANES, key_column, -1)
        send_k[part] = jnp.max(found, axis=0, keepdims=True)

    embeds = embeds_ref[...]
    squares = jnp.sum(embeds * embeds, axis=1, keepdims=True)
    unit = (embeds * lax.rsqrt(squares + 1e-06)).astype(jnp.bfloat16)
    chunk_row = lax.broadcasted_iota(jnp.int32, (LANES, rows), 0)

    for index, chunk in enumerate(order):
        pick = (slot == chunk_row + chunk * LANES).astype(jnp.float32).astype(jnp.bfloat16)
        placed = jnp.dot(pick, unit, preferred_element_type=jnp.float32).astype(jnp.bfloat16)
        send_u[pl.ds(chunk * per, per)] = placed.reshape(per, sub, width)
        if index == 0:
            pl.semaphore_wait(barrier, devices - 1)

        def launch(k, carry, chunk=chunk):
            device = chunk * per + lax.rem(my_place + k, per)
            copy_keys(device).start()
            copy_units(device).start()
            return carry

        lax.fori_loop(1 if index == chunks - 1 else 0, per, launch, 0)

    recv_u[me] = send_u[me]
    recv_k[me] = send_k[my_chunk]

    others(lambda d: await_from(d)(recv_k, k_send, k_recv))
    offset = my_place * sub
    key_rows = []
    place_lane = lax.broadcasted_iota(jnp.int32, (per, LANES), 1)
    place_row = lax.broadcasted_iota(jnp.int32, (per, LANES), 0)
    in_place = (place_lane >= place_row * sub) & (place_lane < place_row * sub + sub)
    for part in range(chunks):
        block = recv_k[part * per:(part + 1) * per].reshape(per, LANES)
        block = pltpu.roll(pltpu.roll(block, lax.rem(LANES - offset, LANES), 1), 0, 1, stride=sub, stride_axis=0)
        key_rows.append(jnp.max(jnp.where(in_place, block, -1), axis=0, keepdims=True))
    keys = jnp.concatenate(key_rows, axis=1)
    keys_column = columns(keys)

    others(lambda d: await_from(d)(recv_u, u_send, u_recv))
    panel = recv_u[...].reshape(slots, width)
    for index, chunk in enumerate(order):
        queries = recv_u[pl.ds(chunk * per, per)].reshape(LANES, width)
        scores = lax.dot_general(panel, queries, (((1,), (1,)), ((), ())), preferred_element_type=jnp.float32)
        query_keys = jnp.full((1, LANES), -1, jnp.int32)
        for part in range(chunks):
            query_keys = jnp.where(chunk == part, key_rows[part], query_keys)
        first = query_keys & (-(1 << bits))
        mask = (keys_column < query_keys) & (keys_column >= first)
        answers[chunk] = jnp.max(jnp.where(mask, scores, -1.0), axis=0, keepdims=True)

        def answer(k, carry, chunk=chunk):
            copy_answers(chunk * per + lax.rem(my_place + k, per)).start()
            return carry

        lax.fori_loop(1 if index == chunks - 1 else 0, per, answer, 0)

    returned[me] = answers[my_chunk]
    others(lambda d: await_from(d)(returned, a_send, a_recv))
    gathered = returned[...].reshape(devices, LANES)
    device_row = lax.broadcasted_iota(jnp.int32, (devices, rows), 0)
    from_bucket = (device_row == bucket).astype(jnp.float32)
    spread = lax.dot_general(
        gathered, from_bucket, (((0,), (0,)), ((), ())),
        precision=lax.Precision.HIGHEST, preferred_element_type=jnp.float32)
    want = position + offset
    out_ref[...] = jnp.sum(jnp.where(chunk_row == want, spread, 0.0), axis=0, keepdims=True)

    def finish(d):
        copy_keys(d).wait_send()
        copy_units(d).wait_send()
        copy_answers(d).wait_send()

    others(finish)


def kernel_body(shards, pairs, embeds, cluster, rank):
    rows, width = embeds.shape
    devices = shards * pairs
    sub = 2 * rows // devices
    bits = log2(devices * rows)
    per = LANES // sub
    chunks = devices // per
    vmem = pl.BlockSpec(memory_space=pltpu.VMEM)
    best = pl.pallas_call(
        functools.partial(kernel, pairs, sub, bits, log2(CL_OWN // pairs)),
        out_shape=jax.ShapeDtypeStruct((1, rows), jnp.float32),
        in_specs=[vmem] * 3,
        out_specs=vmem,
        scratch_shapes=[
            pltpu.VMEM((devices, sub, width), jnp.bfloat16),
            pltpu.VMEM((devices, sub, width), jnp.bfloat16),
            pltpu.VMEM((chunks, 1, LANES), jnp.int32),
            pltpu.VMEM((devices, 1, LANES), jnp.int32),
            pltpu.VMEM((chunks, 1, LANES), jnp.float32),
            pltpu.VMEM((devices, 1, LANES), jnp.float32),
        ] + [pltpu.SemaphoreType.DMA((devices,))] * 6,
        compiler_params=pltpu.CompilerParams(collective_id=0, has_side_effects=True),
    )(embeds, cluster.reshape(1, rows), rank.reshape(1, rows))
    return best.reshape(rows)


def plain_body(embeds, cluster, rank):
    rows, width = embeds.shape
    pairs = lax.axis_size("pair")
    devices = lax.axis_size("shard") * pairs
    sub = 2 * rows // devices
    slots = devices * sub
    squares = jnp.sum(embeds * embeds, axis=1, keepdims=True)
    unit_rows = (embeds * lax.rsqrt(squares + 1e-06)).astype(jnp.bfloat16)
    bucket = cluster // CL_OWN * pairs + cluster % CL_OWN * pairs // CL_OWN
    index = jnp.arange(rows, dtype=jnp.int32)
    before = (bucket[:, None] == bucket[None, :]) & (index[None, :] < index[:, None])
    slot = bucket * sub + jnp.sum(before.astype(jnp.int32), axis=1)

    def exchange(array):
        blocks = array.reshape((devices, sub) + array.shape[1:])
        return lax.all_to_all(blocks, ("shard", "pair"), 0, 0, tiled=True).reshape(array.shape)

    units = exchange(jnp.zeros((slots, width), jnp.bfloat16).at[slot].set(unit_rows))
    clusters = exchange(jnp.full((slots,), -1, jnp.int32).at[slot].set(cluster))
    ranks = exchange(jnp.zeros((slots,), jnp.int32).at[slot].set(rank))
    scores = jnp.einsum("qd,kd->qk", units, units, preferred_element_type=jnp.float32)
    mask = (clusters[:, None] == clusters[None, :]) & (ranks[None, :] < ranks[:, None])
    return exchange(jnp.max(jnp.where(mask, scores, -1.0), axis=1))[slot]


def solution(mesh):
    shards, pairs = mesh.shape["shard"], mesh.shape["pair"]
    devices = shards * pairs

    def body(embeds, cluster, rank):
        rows, width = embeds.shape
        sub = 2 * rows // devices
        quarter = CL_OWN // pairs
        fits = (
            CL_OWN % pairs == 0 and quarter & (quarter - 1) == 0
            and sub % 16 == 0 and LANES % sub == 0 and devices % (LANES // sub) == 0
            and rows % LANES == 0 and width % LANES == 0
        )
        if fits:
            return kernel_body(shards, pairs, embeds, cluster, rank)
        return plain_body(embeds, cluster, rank)

    in_specs = (P(("shard", "pair"), None), P(("shard", "pair")), P(("shard", "pair")))
    return jax.shard_map(body, mesh=mesh, in_specs=in_specs, out_specs=P(("shard", "pair")), check_vma=False)
```

```python
import functools

import jax
import jax.numpy as jnp
from jax import lax
from jax.experimental import pallas as pl
from jax.experimental.pallas import tpu as pltpu
from jax.sharding import PartitionSpec as P

CL_OWN = 16
LANES = 128
MESH = pl.DeviceIdType.MESH


def log2(value):
    return (value - 1).bit_length()


def kernel(
    pairs, sub, bits, step_bits,
    embeds_in, cluster_in, rank_in, out_ref,
    embeds_ref, cluster_ref, rank_ref,
    send_u, recv_u, send_k, recv_k, answers, returned,
    u_send, u_recv, k_send, k_recv, a_send, a_recv, in_sems, complete,
):
    devices = recv_u.shape[0]
    rows, width = embeds_ref.shape
    slots = devices * sub
    per = LANES // sub
    chunks = devices // per
    me = lax.axis_index("shard") * pairs + lax.axis_index("pair")
    my_chunk = me // per
    my_place = me % per

    def coords(device):
        return (device // pairs, device % pairs)

    def copy_units(device):
        return pltpu.make_async_remote_copy(
            src_ref=send_u.at[device], dst_ref=recv_u.at[me],
            send_sem=u_send.at[device], recv_sem=u_recv.at[me],
            device_id=coords(device), device_id_type=MESH)

    def copy_keys(device):
        return pltpu.make_async_remote_copy(
            src_ref=send_k.at[device // per], dst_ref=recv_k.at[me],
            send_sem=k_send.at[device], recv_sem=k_recv.at[me],
            device_id=coords(device), device_id_type=MESH)

    def copy_answers(device):
        return pltpu.make_async_remote_copy(
            src_ref=answers.at[device // per], dst_ref=returned.at[me],
            send_sem=a_send.at[device], recv_sem=a_recv.at[me],
            device_id=coords(device), device_id_type=MESH)

    def await_from(device):
        def wait(buffer, send, recv):
            pltpu.make_async_remote_copy(
                src_ref=buffer.at[device], dst_ref=buffer.at[device],
                send_sem=send.at[device], recv_sem=recv.at[device],
                device_id=coords(device), device_id_type=MESH).wait_recv()
        return wait

    def others(action):
        def step(k, carry):
            action(lax.rem(me + k, devices))
            return carry
        lax.fori_loop(1, devices, step, 0)

    if chunks == 4:
        order = [3 - my_chunk, (my_chunk + 2) % 4, my_chunk + 1 - 2 * (my_chunk % 2), my_chunk]
    else:
        order = [(my_chunk + chunks // 2 + k) % chunks for k in range(chunks)]

    barrier = pltpu.get_barrier_semaphore()
    line, side = my_place // 2, my_place % 2
    lines = per // 2

    def on_line(k):
        spot = lax.rem(my_chunk * 2 + side + k, 2 * chunks)
        return (spot // 2) * per + line * 2 + spot % 2

    def beside(k):
        return my_chunk * per + lax.rem(line + k, lines) * 2 + side

    def signal(semaphore, device):
        pl.semaphore_signal(semaphore, inc=1, device_id=coords(device), device_id_type=MESH)

    def run(start, stop, action):
        def step(k, carry):
            action(k)
            return carry
        lax.fori_loop(start, stop, step, 0)

    run(1, 2 * chunks, lambda k: signal(barrier, on_line(k)))
    run(1, lines, lambda k: signal(barrier, beside(k)))

    loads = [
        pltpu.make_async_copy(source, target, in_sems.at[k])
        for k, (source, target) in enumerate(
            [(cluster_in, cluster_ref), (rank_in, rank_ref), (embeds_in, embeds_ref)])
    ]
    for load in loads:
        load.start()
    loads[0].wait()
    loads[1].wait()
    cluster = cluster_ref[...]
    key = cluster * (1 << bits) + rank_ref[...]
    bucket = lax.shift_right_logical(cluster, step_bits)

    def columns(row):
        return jnp.transpose(jnp.broadcast_to(row, (LANES, row.shape[1])))

    bucket_column = columns(bucket)
    lower = lax.broadcasted_iota(jnp.int32, (rows, LANES), 0)
    lane = lax.broadcasted_iota(jnp.int32, (rows, LANES), 1)
    places = []
    for part in range(rows // LANES):
        here = bucket[:, part * LANES:(part + 1) * LANES]
        before = (bucket_column == here) & (lower < lane + part * LANES)
        places.append(jnp.sum(before.astype(jnp.int32), axis=0, keepdims=True))
    position = jnp.concatenate(places, axis=1)
    slot = bucket * sub + position
    slot_column = columns(slot)
    key_column = columns(key)
    for part in range(chunks):
        found = jnp.where(slot_column == lane + part * LANES, key_column, -1)
        send_k[part] = jnp.max(found, axis=0, keepdims=True)

    loads[2].wait()
    embeds = embeds_ref[...]
    squares = jnp.sum(embeds * embeds, axis=1, keepdims=True)
    unit = (embeds * lax.rsqrt(squares + 1e-06)).astype(jnp.bfloat16)
    chunk_row = lax.broadcasted_iota(jnp.int32, (LANES, rows), 0)

    def send(device):
        copy_keys(device).start()
        copy_units(device).start()

    def place(chunk):
        pick = (slot == chunk_row + chunk * LANES).astype(jnp.float32).astype(jnp.bfloat16)
        placed = jnp.dot(pick, unit, preferred_element_type=jnp.float32).astype(jnp.bfloat16)
        send_u[pl.ds(chunk * per, per)] = placed.reshape(per, sub, width)

    early = chunks // 2
    for chunk in order[:early]:
        place(chunk)
    pl.semaphore_wait(barrier, 2 * chunks - 1 + lines - 1)
    run(1, lines, lambda k: signal(complete, beside(k)))
    for chunk in order[:early]:
        run(0, 2, lambda k, chunk=chunk: send(chunk * per + line * 2 + lax.rem(side + k, 2)))
    for chunk in order[early:]:
        place(chunk)
    pl.semaphore_wait(complete, lines - 1)
    for index, chunk in enumerate(order):
        first = 2 if index < early else 1 if index == chunks - 1 else 0
        base = my_place if index == chunks - 1 else line * 2
        run(first, per, lambda k, chunk=chunk, base=base: send(chunk * per + lax.rem(base + k, per)))

    recv_u[me] = send_u[me]
    recv_k[me] = send_k[my_chunk]

    others(lambda d: await_from(d)(recv_k, k_send, k_recv))
    offset = my_place * sub
    key_rows = []
    place_lane = lax.broadcasted_iota(jnp.int32, (per, LANES), 1)
    place_row = lax.broadcasted_iota(jnp.int32, (per, LANES), 0)
    in_place = (place_lane >= place_row * sub) & (place_lane < place_row * sub + sub)
    for part in range(chunks):
        block = recv_k[part * per:(part + 1) * per].reshape(per, LANES)
        block = pltpu.roll(pltpu.roll(block, lax.rem(LANES - offset, LANES), 1), 0, 1, stride=sub, stride_axis=0)
        key_rows.append(jnp.max(jnp.where(in_place, block, -1), axis=0, keepdims=True))
    keys = jnp.concatenate(key_rows, axis=1)
    keys_column = columns(keys)

    others(lambda d: await_from(d)(recv_u, u_send, u_recv))
    panel = recv_u[...].reshape(slots, width)
    for index, chunk in enumerate(order):
        queries = recv_u[pl.ds(chunk * per, per)].reshape(LANES, width)
        scores = lax.dot_general(panel, queries, (((1,), (1,)), ((), ())), preferred_element_type=jnp.float32)
        query_keys = jnp.full((1, LANES), -1, jnp.int32)
        for part in range(chunks):
            query_keys = jnp.where(chunk == part, key_rows[part], query_keys)
        first = query_keys & (-(1 << bits))
        mask = (keys_column < query_keys) & (keys_column >= first)
        answers[chunk] = jnp.max(jnp.where(mask, scores, -1.0), axis=0, keepdims=True)

        def answer(k, carry, chunk=chunk):
            copy_answers(chunk * per + lax.rem(my_place + k, per)).start()
            return carry

        lax.fori_loop(1 if index == chunks - 1 else 0, per, answer, 0)

    returned[me] = answers[my_chunk]
    others(lambda d: await_from(d)(returned, a_send, a_recv))
    gathered = returned[...].reshape(devices, LANES)
    device_row = lax.broadcasted_iota(jnp.int32, (devices, rows), 0)
    from_bucket = (device_row == bucket).astype(jnp.float32)
    spread = lax.dot_general(
        gathered, from_bucket, (((0,), (0,)), ((), ())),
        precision=lax.Precision.HIGHEST, preferred_element_type=jnp.float32)
    want = position + offset
    out_ref[...] = jnp.sum(jnp.where(chunk_row == want, spread, 0.0), axis=0, keepdims=True)

    def finish(d):
        copy_keys(d).wait_send()
        copy_units(d).wait_send()
        copy_answers(d).wait_send()

    others(finish)


def kernel_body(shards, pairs, embeds, cluster, rank):
    rows, width = embeds.shape
    devices = shards * pairs
    sub = 2 * rows // devices
    bits = log2(devices * rows)
    per = LANES // sub
    chunks = devices // per
    vmem = pl.BlockSpec(memory_space=pltpu.VMEM)
    best = pl.pallas_call(
        functools.partial(kernel, pairs, sub, bits, log2(CL_OWN // pairs)),
        out_shape=jax.ShapeDtypeStruct((1, rows), jnp.float32),
        in_specs=[pl.BlockSpec(memory_space=pl.ANY)] * 3,
        out_specs=vmem,
        scratch_shapes=[
            pltpu.VMEM((rows, width), jnp.float32),
            pltpu.VMEM((1, rows), jnp.int32),
            pltpu.VMEM((1, rows), jnp.int32),
            pltpu.VMEM((devices, sub, width), jnp.bfloat16),
            pltpu.VMEM((devices, sub, width), jnp.bfloat16),
            pltpu.VMEM((chunks, 1, LANES), jnp.int32),
            pltpu.VMEM((devices, 1, LANES), jnp.int32),
            pltpu.VMEM((chunks, 1, LANES), jnp.float32),
            pltpu.VMEM((devices, 1, LANES), jnp.float32),
        ] + [pltpu.SemaphoreType.DMA((devices,))] * 6
        + [pltpu.SemaphoreType.DMA((3,)), pltpu.SemaphoreType.REGULAR],
        compiler_params=pltpu.CompilerParams(collective_id=0, has_side_effects=True),
    )(embeds, cluster.reshape(1, rows), rank.reshape(1, rows))
    return best.reshape(rows)


def plain_body(embeds, cluster, rank):
    rows, width = embeds.shape
    pairs = lax.axis_size("pair")
    devices = lax.axis_size("shard") * pairs
    sub = 2 * rows // devices
    slots = devices * sub
    squares = jnp.sum(embeds * embeds, axis=1, keepdims=True)
    unit_rows = (embeds * lax.rsqrt(squares + 1e-06)).astype(jnp.bfloat16)
    bucket = cluster // CL_OWN * pairs + cluster % CL_OWN * pairs // CL_OWN
    index = jnp.arange(rows, dtype=jnp.int32)
    before = (bucket[:, None] == bucket[None, :]) & (index[None, :] < index[:, None])
    slot = bucket * sub + jnp.sum(before.astype(jnp.int32), axis=1)

    def exchange(array):
        blocks = array.reshape((devices, sub) + array.shape[1:])
        return lax.all_to_all(blocks, ("shard", "pair"), 0, 0, tiled=True).reshape(array.shape)

    units = exchange(jnp.zeros((slots, width), jnp.bfloat16).at[slot].set(unit_rows))
    clusters = exchange(jnp.full((slots,), -1, jnp.int32).at[slot].set(cluster))
    ranks = exchange(jnp.zeros((slots,), jnp.int32).at[slot].set(rank))
    scores = jnp.einsum("qd,kd->qk", units, units, preferred_element_type=jnp.float32)
    mask = (clusters[:, None] == clusters[None, :]) & (ranks[None, :] < ranks[:, None])
    return exchange(jnp.max(jnp.where(mask, scores, -1.0), axis=1))[slot]


def solution(mesh):
    shards, pairs = mesh.shape["shard"], mesh.shape["pair"]
    devices = shards * pairs

    def body(embeds, cluster, rank):
        rows, width = embeds.shape
        sub = 2 * rows // devices
        quarter = CL_OWN // pairs
        fits = (
            CL_OWN % pairs == 0 and quarter & (quarter - 1) == 0
            and sub % 16 == 0 and LANES % sub == 0 and devices % (LANES // sub) == 0
            and rows % LANES == 0 and width % LANES == 0
        )
        if fits:
            return kernel_body(shards, pairs, embeds, cluster, rank)
        return plain_body(embeds, cluster, rank)

    in_specs = (P(("shard", "pair"), None), P(("shard", "pair")), P(("shard", "pair")))
    return jax.shard_map(body, mesh=mesh, in_specs=in_specs, out_specs=P(("shard", "pair")), check_vma=False)
```

```python
import functools

import jax
import jax.numpy as jnp
from jax import lax
from jax.experimental import pallas as pl
from jax.experimental.pallas import tpu as pltpu
from jax.sharding import PartitionSpec as P

CL_OWN = 16
LANES = 128
MESH = pl.DeviceIdType.MESH


def log2(value):
    return (value - 1).bit_length()


def kernel(
    pairs, sub, bits, step_bits,
    embeds_in, cluster_in, rank_in, out_ref,
    embeds_ref, cluster_ref, rank_ref,
    send_u, recv_u, send_k, recv_k, answers, returned,
    u_send, u_recv, k_send, k_recv, a_send, a_recv, in_sems, complete,
):
    devices = recv_u.shape[0]
    rows, width = embeds_ref.shape
    slots = devices * sub
    per = LANES // sub
    chunks = devices // per
    me = lax.axis_index("shard") * pairs + lax.axis_index("pair")
    my_chunk = me // per
    my_place = me % per

    def coords(device):
        return (device // pairs, device % pairs)

    def copy_units(device):
        return pltpu.make_async_remote_copy(
            src_ref=send_u.at[device], dst_ref=recv_u.at[me],
            send_sem=u_send.at[device], recv_sem=u_recv.at[me],
            device_id=coords(device), device_id_type=MESH)

    def copy_keys(device):
        return pltpu.make_async_remote_copy(
            src_ref=send_k.at[device // per], dst_ref=recv_k.at[me],
            send_sem=k_send.at[device], recv_sem=k_recv.at[me],
            device_id=coords(device), device_id_type=MESH)

    def copy_answers(device):
        return pltpu.make_async_remote_copy(
            src_ref=answers.at[device // per], dst_ref=returned.at[me],
            send_sem=a_send.at[device], recv_sem=a_recv.at[me],
            device_id=coords(device), device_id_type=MESH)

    def await_from(device):
        def wait(buffer, send, recv):
            pltpu.make_async_remote_copy(
                src_ref=buffer.at[device], dst_ref=buffer.at[device],
                send_sem=send.at[device], recv_sem=recv.at[device],
                device_id=coords(device), device_id_type=MESH).wait_recv()
        return wait

    def others(action):
        def step(k, carry):
            action(lax.rem(me + k, devices))
            return carry
        lax.fori_loop(1, devices, step, 0)

    order = [3 - my_chunk, (my_chunk + 2) % 4, my_chunk + 1 - 2 * (my_chunk % 2), my_chunk]

    barrier = pltpu.get_barrier_semaphore()
    line, side = my_place // 2, my_place % 2
    lines = per // 2

    def on_line(k):
        spot = lax.rem(my_chunk * 2 + side + k, 2 * chunks)
        return (spot // 2) * per + line * 2 + spot % 2

    def beside(k):
        return my_chunk * per + lax.rem(line + k, lines) * 2 + side

    def signal(semaphore, device):
        pl.semaphore_signal(semaphore, inc=1, device_id=coords(device), device_id_type=MESH)

    def run(start, stop, action):
        def step(k, carry):
            action(k)
            return carry
        lax.fori_loop(start, stop, step, 0)

    run(1, 2 * chunks, lambda k: signal(barrier, on_line(k)))
    run(1, lines, lambda k: signal(barrier, beside(k)))

    loads = [
        pltpu.make_async_copy(source, target, in_sems.at[k])
        for k, (source, target) in enumerate(
            [(cluster_in, cluster_ref), (rank_in, rank_ref), (embeds_in, embeds_ref)])
    ]
    for load in loads:
        load.start()
    loads[0].wait()
    loads[1].wait()
    cluster = cluster_ref[...]
    key = cluster * (1 << bits) + rank_ref[...]
    bucket = lax.shift_right_logical(cluster, step_bits)

    def columns(row):
        return jnp.transpose(jnp.broadcast_to(row, (LANES, row.shape[1])))

    bucket_column = columns(bucket)
    lower = lax.broadcasted_iota(jnp.int32, (rows, LANES), 0)
    lane = lax.broadcasted_iota(jnp.int32, (rows, LANES), 1)
    places = []
    for part in range(rows // LANES):
        here = bucket[:, part * LANES:(part + 1) * LANES]
        before = (bucket_column == here) & (lower < lane + part * LANES)
        places.append(jnp.sum(before.astype(jnp.int32), axis=0, keepdims=True))
    position = jnp.concatenate(places, axis=1)
    slot = bucket * sub + position
    slot_column = columns(slot)
    key_column = columns(key)
    for part in range(chunks):
        found = jnp.where(slot_column == lane + part * LANES, key_column, -1)
        send_k[part] = jnp.max(found, axis=0, keepdims=True)

    loads[2].wait()
    embeds = embeds_ref[...]
    squares = jnp.sum(embeds * embeds, axis=1, keepdims=True)
    unit = (embeds * lax.rsqrt(squares + 1e-06)).astype(jnp.bfloat16)
    chunk_row = lax.broadcasted_iota(jnp.int32, (LANES, rows), 0)

    def send(device):
        copy_keys(device).start()
        copy_units(device).start()

    def place(chunk):
        pick = (slot == chunk_row + chunk * LANES).astype(jnp.float32).astype(jnp.bfloat16)
        placed = jnp.dot(pick, unit, preferred_element_type=jnp.float32).astype(jnp.bfloat16)
        send_u[pl.ds(chunk * per, per)] = placed.reshape(per, sub, width)

    early = chunks // 2
    for chunk in order[:early]:
        place(chunk)
    pl.semaphore_wait(barrier, 2 * chunks - 1 + lines - 1)
    run(1, lines, lambda k: signal(complete, beside(k)))
    for chunk in order[:early]:
        run(0, 2, lambda k, chunk=chunk: send(chunk * per + line * 2 + lax.rem(side + k, 2)))
    for chunk in order[early:]:
        place(chunk)
    pl.semaphore_wait(complete, lines - 1)
    for index, chunk in enumerate(order):
        first = 2 if index < early else 1 if index == chunks - 1 else 0
        base = my_place if index == chunks - 1 else line * 2
        run(first, per, lambda k, chunk=chunk, base=base: send(chunk * per + lax.rem(base + k, per)))

    recv_u[me] = send_u[me]
    recv_k[me] = send_k[my_chunk]

    others(lambda d: await_from(d)(recv_k, k_send, k_recv))
    offset = my_place * sub
    key_rows = []
    place_lane = lax.broadcasted_iota(jnp.int32, (per, LANES), 1)
    place_row = lax.broadcasted_iota(jnp.int32, (per, LANES), 0)
    in_place = (place_lane >= place_row * sub) & (place_lane < place_row * sub + sub)
    for part in range(chunks):
        block = recv_k[part * per:(part + 1) * per].reshape(per, LANES)
        block = pltpu.roll(pltpu.roll(block, lax.rem(LANES - offset, LANES), 1), 0, 1, stride=sub, stride_axis=0)
        key_rows.append(jnp.max(jnp.where(in_place, block, -1), axis=0, keepdims=True))

    def await_units(chunk, mine):
        def step(k, carry):
            await_from(chunk * per + lax.rem(my_place + k, per))(recv_u, u_send, u_recv)
            return carry
        lax.fori_loop(1 if mine else 0, per, step, 0)

    def keys_of(chunk):
        row = jnp.full((1, LANES), -1, jnp.int32)
        for part in range(chunks):
            row = jnp.where(chunk == part, key_rows[part], row)
        return row

    def block(chunk):
        return recv_u[pl.ds(chunk * per, per)].reshape(LANES, width)

    def best_of(panel, panel_keys, queries, query_keys):
        scores = lax.dot_general(panel, queries, (((1,), (1,)), ((), ())), preferred_element_type=jnp.float32)
        first = query_keys & (-(1 << bits))
        mask = (panel_keys < query_keys) & (panel_keys >= first)
        return jnp.max(jnp.where(mask, scores, -1.0), axis=0, keepdims=True)

    last = order[1]
    ready = order[2:] + order[:1]
    for chunk in reversed(ready[:-1]):
        await_units(chunk, chunk is order[-1])
    await_units(order[0], False)
    ready_rows = jnp.concatenate([block(c) for c in ready], axis=0)
    ready_keys = jnp.concatenate([columns(keys_of(c)) for c in ready], axis=0)
    partial = [best_of(ready_rows, ready_keys, block(c), keys_of(c)) for c in ready]
    for index, found in enumerate(partial):
        answers[ready[index]] = found
    await_units(last, False)
    last_rows, last_keys = block(last), keys_of(last)
    last_column = columns(last_keys)

    def answer_to(chunk, mine):
        def step(k, carry):
            copy_answers(chunk * per + lax.rem(my_place + k, per)).start()
            return carry
        lax.fori_loop(1 if mine else 0, per, step, 0)

    def complete_answer(chunk, mine):
        more = best_of(last_rows, last_column, block(chunk), keys_of(chunk))
        answers[chunk] = jnp.maximum(answers[chunk], more)
        answer_to(chunk, mine)

    complete_answer(order[0], False)
    here = best_of(last_rows, last_column, last_rows, last_keys)
    answers[last] = jnp.maximum(here, best_of(ready_rows, ready_keys, last_rows, last_keys))
    answer_to(last, False)
    for chunk in order[2:]:
        complete_answer(chunk, chunk is order[-1])

    returned[me] = answers[my_chunk]

    def finish(d):
        copy_keys(d).wait_send()
        copy_units(d).wait_send()
        copy_answers(d).wait_send()

    others(finish)
    others(lambda d: await_from(d)(returned, a_send, a_recv))
    gathered = returned[...].reshape(devices, LANES)
    device_row = lax.broadcasted_iota(jnp.int32, (devices, rows), 0)
    from_bucket = (device_row == bucket).astype(jnp.float32)
    spread = lax.dot_general(
        gathered, from_bucket, (((0,), (0,)), ((), ())),
        precision=lax.Precision.HIGHEST, preferred_element_type=jnp.float32)
    want = position + offset
    out_ref[...] = jnp.sum(jnp.where(chunk_row == want, spread, 0.0), axis=0, keepdims=True)


def kernel_body(shards, pairs, embeds, cluster, rank):
    rows, width = embeds.shape
    devices = shards * pairs
    sub = 2 * rows // devices
    bits = log2(devices * rows)
    per = LANES // sub
    chunks = devices // per
    vmem = pl.BlockSpec(memory_space=pltpu.VMEM)
    best = pl.pallas_call(
        functools.partial(kernel, pairs, sub, bits, log2(CL_OWN // pairs)),
        out_shape=pltpu.VMEM((1, rows), jnp.float32),
        in_specs=[pl.BlockSpec(memory_space=pl.ANY)] * 3,
        out_specs=vmem,
        scratch_shapes=[
            pltpu.VMEM((rows, width), jnp.float32),
            pltpu.VMEM((1, rows), jnp.int32),
            pltpu.VMEM((1, rows), jnp.int32),
            pltpu.VMEM((devices, sub, width), jnp.bfloat16),
            pltpu.VMEM((devices, sub, width), jnp.bfloat16),
            pltpu.VMEM((chunks, 1, LANES), jnp.int32),
            pltpu.VMEM((devices, 1, LANES), jnp.int32),
            pltpu.VMEM((chunks, 1, LANES), jnp.float32),
            pltpu.VMEM((devices, 1, LANES), jnp.float32),
        ] + [pltpu.SemaphoreType.DMA((devices,))] * 6
        + [pltpu.SemaphoreType.DMA((3,)), pltpu.SemaphoreType.REGULAR],
        compiler_params=pltpu.CompilerParams(collective_id=0, has_side_effects=True),
    )(embeds, cluster.reshape(1, rows), rank.reshape(1, rows))
    return best.reshape(rows)


def plain_body(embeds, cluster, rank):
    rows, width = embeds.shape
    pairs = lax.axis_size("pair")
    devices = lax.axis_size("shard") * pairs
    sub = 2 * rows // devices
    slots = devices * sub
    squares = jnp.sum(embeds * embeds, axis=1, keepdims=True)
    unit_rows = (embeds * lax.rsqrt(squares + 1e-06)).astype(jnp.bfloat16)
    bucket = cluster // CL_OWN * pairs + cluster % CL_OWN * pairs // CL_OWN
    index = jnp.arange(rows, dtype=jnp.int32)
    before = (bucket[:, None] == bucket[None, :]) & (index[None, :] < index[:, None])
    slot = bucket * sub + jnp.sum(before.astype(jnp.int32), axis=1)

    def exchange(array):
        blocks = array.reshape((devices, sub) + array.shape[1:])
        return lax.all_to_all(blocks, ("shard", "pair"), 0, 0, tiled=True).reshape(array.shape)

    units = exchange(jnp.zeros((slots, width), jnp.bfloat16).at[slot].set(unit_rows))
    clusters = exchange(jnp.full((slots,), -1, jnp.int32).at[slot].set(cluster))
    ranks = exchange(jnp.zeros((slots,), jnp.int32).at[slot].set(rank))
    scores = jnp.einsum("qd,kd->qk", units, units, preferred_element_type=jnp.float32)
    mask = (clusters[:, None] == clusters[None, :]) & (ranks[None, :] < ranks[:, None])
    return exchange(jnp.max(jnp.where(mask, scores, -1.0), axis=1))[slot]


def solution(mesh):
    shards, pairs = mesh.shape["shard"], mesh.shape["pair"]
    devices = shards * pairs

    def body(embeds, cluster, rank):
        rows, width = embeds.shape
        sub = 2 * rows // devices
        quarter = CL_OWN // pairs
        fits = (
            CL_OWN % pairs == 0 and quarter & (quarter - 1) == 0
            and sub % 16 == 0 and LANES % sub == 0 and devices == 4 * (LANES // sub)
            and rows % LANES == 0 and width % LANES == 0
        )
        if fits:
            return kernel_body(shards, pairs, embeds, cluster, rank)
        return plain_body(embeds, cluster, rank)

    in_specs = (P(("shard", "pair"), None), P(("shard", "pair")), P(("shard", "pair")))
    return jax.shard_map(body, mesh=mesh, in_specs=in_specs, out_specs=P(("shard", "pair")), check_vma=False)
```
